32 devices in a mesh: expert: 8 (over z, y), dp: 4 (over x, core).
Axes of the slice: x: 2, y: 2, z: 4, core: 2. Of those that a mesh axis runs over, the one named last changes fastest.
Arguments:
- features: bfloat16 [32, 3072, 256], P(('expert', 'dp')), may hold values from -6 to 6
- expert_of: int32 [32, 3072, 1], P(('expert', 'dp')), may hold values from 0 to 127, as said below
- segment_of: int32 [32, 3072], P(('expert', 'dp')), may hold values from 0 to 47, never falling along the last dimension, each value on 1 to 128 neighbouring positions
- step_len: float32 [32, 3072], P(('expert', 'dp')), may hold values from 0.005 to 0.05
- target: float32 [32, 3072], P(('expert', 'dp')), may hold values from -6 to 6
- w_first: bfloat16 [128, 256, 256], P(('expert', 'dp')), may hold values from -0.375 to 0.375
- w_second: bfloat16 [128, 256, 256], P(('expert', 'dp')), may hold values from -0.375 to 0.375
- w_head: bfloat16 [128, 256], P(('expert', 'dp')), may hold values from -1.25 to 1.25
Outputs:
- extinction: float32 [32, 3072], P(('expert', 'dp'))
- grad_first: bfloat16 [128, 256, 256], P(('expert', 'dp'))
- grad_second: bfloat16 [128, 256, 256], P(('expert', 'dp'))
- grad_head: bfloat16 [128, 256], P(('expert', 'dp'))
The draws below stay inside these ranges and needn't reach their ends.
Inputs may be any that keep to these rules, and one draw needn't show every extreme that they name: `expert_of`: experts e * 4 to e * 4 + 3 lie on device e. On every device, no expert is named by more than 48 samples and one is named by exactly 48; the experts of no one device are named by more than 144 samples together, and those of one device by exactly 144. `segment_of`: within a device, sightline numbers never fall along the samples; each sightline has 1 to 128 samples and one has exactly 128.
All inputs are finite; a program needn't handle non-finite values.
Results may differ from the reference program's by a relative error of at most 0.0059.
Values may be sent and summed in bfloat16 or wider, within the bound.
A program may use at most 128 MiB of HBM per device.

```python
import math
import jax
import jax.numpy as jnp
import numpy as np
from jax import lax

ENC = 256
HID = 256
EXP_DEV = 4
SEG_MOST = 128
S_DEV = 3072
SIGHT = 48
SHARDS = 32
EXPERTS = 128
CAP = 48
DEST_CAP = 144


def routes_one_device(key):
    total_slots = SHARDS * DEST_CAP
    key_full, key_order, key_offset, key_shuffle = jax.random.split(key, 4)
    full_dest = jax.random.randint(key_full, (), 0, SHARDS).astype(jnp.int32)
    slots = jnp.arange(total_slots, dtype=jnp.int32)
    slot_dest = slots // DEST_CAP
    slot_pos = slots % DEST_CAP
    priority = jax.random.permutation(key_order, total_slots).astype(jnp.int32)
    scores = jnp.where(slot_dest == full_dest, -1, priority).astype(jnp.int32)
    chosen = jnp.argsort(scores, stable=True).astype(jnp.int32)[:S_DEV]
    offsets = jax.random.randint(key_offset, (SHARDS,), 0, EXP_DEV).astype(jnp.int32)
    others = max(EXP_DEV - 1, 1)
    chosen_dest = slot_dest[chosen]
    chosen_pos = slot_pos[chosen]
    step_of = jnp.where(chosen_pos < CAP, 0, 1 + (chosen_pos - CAP) % others).astype(jnp.int32)
    local = (offsets[chosen_dest] + step_of) % EXP_DEV
    experts_named = (chosen_dest * EXP_DEV + local).astype(jnp.int32)
    shuffle = jax.random.permutation(key_shuffle, S_DEV).astype(jnp.int32)
    return experts_named[shuffle]


def draw_expert_of(key, part):
    keys = jax.vmap(lambda index: jax.random.fold_in(jax.random.fold_in(key, 7919), index))(jnp.arange(SHARDS, dtype=jnp.int32))
    return jax.vmap(routes_one_device)(keys)[:, :, None].astype(jnp.int32)


def block_scale(own_key, shape, pieces, least, high):
    level, own = 1.0, jax.random.fold_in(own_key, 6)
    for dim, shards_of in pieces:
        draws = jnp.exp(jax.random.uniform(jax.random.fold_in(own, dim), (shards_of,), jnp.float32, least / len(pieces), high / len(pieces)))
        level = level * jnp.repeat(draws, shape[dim] // shards_of).reshape([-1 if axis == dim else 1 for axis in range(len(shape))])
    return level


def length_profile(count, total, limit, slope):
    weights = [(1 << 20) // math.isqrt(grade ** slope) + 1 for grade in range(2, count + 1)]
    rest, holding = total - limit - (count - 1), [1] * (count - 1)
    while rest > 0:
        candidates = [i for i in range(count - 1) if holding[i] < limit]
        whole, left = sum([weights[i] for i in candidates]), rest
        for i in candidates:
            extra = min(limit - holding[i], max(1, left * weights[i] // whole), rest)
            holding[i] = holding[i] + extra
            rest = rest - extra
    return np.array([limit] + holding)


def ragged_sizes(rng, count, total, limit, skew):
    if count == 2:
        one = jax.random.randint(rng, (), max(1, total - limit), min(limit, total - 1) + 1)
        return jnp.stack([one, total - one])
    sizes = jnp.asarray(length_profile(count, total, limit, skew), jnp.int32)
    couples = (count - 1) // 2
    giver, taker = sizes[1:1 + 2 * couples:2], sizes[2:2 + 2 * couples:2]
    room = jnp.minimum(giver - 1, limit - taker)
    passed = jax.random.randint(jax.random.fold_in(rng, 1), (couples,), 0, 1 << 20) % (room + 1)
    sizes = sizes.at[1:1 + 2 * couples:2].set(giver - passed).at[2:2 + 2 * couples:2].set(taker + passed)
    return sizes[jax.random.permutation(jax.random.fold_in(rng, 2), count)]


def scatter_about(rng, extent, scale, limit, cuts=(), kind=jnp.bfloat16):
    result = scale * jax.random.normal(rng, extent, jnp.float32)
    if cuts:
        result = result * block_scale(rng, extent, cuts, -0.22, 0.18)
    return jnp.clip(result, -limit, limit).astype(kind)


def setup_inputs(seed: int = 0) -> dict:
    key_of = jax.random.split(jax.random.key(seed), 9)
    return {
        "features": scatter_about(key_of[0], (SHARDS, S_DEV, ENC), 1.0, 6.0, ((0, 32),)),
        "expert_of": draw_expert_of(jax.random.fold_in(key_of[8], 71), 0),
        "segment_of": jax.vmap(lambda own: jnp.searchsorted(jnp.cumsum(ragged_sizes(own, SIGHT, S_DEV, SEG_MOST, 1)), jnp.arange(S_DEV), side="right"))(jax.random.split(key_of[2], SHARDS)).reshape((SHARDS, S_DEV)).astype(jnp.int32),
        "step_len": jnp.clip(jnp.exp(math.log(0.05) - 2.3025851 * jax.random.uniform(key_of[3], (SHARDS, S_DEV), jnp.float32) ** block_scale(key_of[3], (SHARDS, S_DEV), ((0, 32),), -0.2, 0.2)), 0.005, 0.05),
        "target": scatter_about(key_of[4], (SHARDS, S_DEV), 1.0, 6.0, ((0, 32),), jnp.float32),
        "w_first": scatter_about(key_of[5], (EXPERTS, ENC, HID), ENC ** -0.5, 0.375, ((0, 32),)),
        "w_second": scatter_about(key_of[6], (EXPERTS, HID, HID), HID ** -0.5, 0.375, ((0, 32),)),
        "w_head": scatter_about(key_of[7], (EXPERTS, HID), 0.2, 1.25, ((0, 32),)),
    }


def silu_slope(values):
    sigma = jax.nn.sigmoid(values)
    return sigma * (1.0 + values * (1.0 - sigma))


def rank_in_device(routes):
    amount = routes.shape[0]
    ordering = jnp.argsort(routes, stable=True).astype(jnp.int32)
    ordered = routes[ordering]
    indices = jnp.arange(amount, dtype=jnp.int32)
    starts = jnp.concatenate([jnp.ones((1,), jnp.bool_), ordered[1:] != ordered[:-1]])
    first_pos = lax.cummax(jnp.where(starts, indices, 0), axis=0)
    return jnp.zeros((amount,), jnp.int32).at[ordering].set(indices - first_pos)


def running_sums(values, segment_ids):
    totals = jax.ops.segment_sum(values, segment_ids, num_segments=SIGHT)
    earlier = jnp.cumsum(totals) - totals
    return jnp.cumsum(values) - earlier[segment_ids], totals[segment_ids]


def forward(inputs, first_mat, second_mat, head_row):
    pre_one = jnp.dot(inputs, first_mat, preferred_element_type=jnp.float32)
    act_one = jax.nn.silu(pre_one).astype(jnp.bfloat16)
    pre_two = jnp.dot(act_one, second_mat, preferred_element_type=jnp.float32)
    act_two = jax.nn.silu(pre_two).astype(jnp.bfloat16)
    logits = jnp.dot(act_two, head_row, preferred_element_type=jnp.float32)
    return pre_one, act_one, pre_two, act_two, logits


def reference(features, expert_of, segment_of, step_len, target, w_first, w_second, w_head):
    shards = segment_of.shape[0]
    routes = expert_of[:, :, 0]
    rank_list = jax.vmap(rank_in_device)(routes)
    device_ids = jnp.arange(shards, dtype=jnp.int32)[:, None]
    per_expert = shards * CAP
    slot_index = (routes * per_expert + device_ids * CAP + rank_list).reshape(-1).astype(jnp.int32)
    sample_count = shards * S_DEV
    lookup = jnp.full((EXPERTS * per_expert,), sample_count, jnp.int32)
    lookup = lookup.at[slot_index].set(jnp.arange(sample_count, dtype=jnp.int32)).reshape(EXPERTS, per_expert)
    padded = jnp.concatenate([features.reshape(sample_count, ENC), jnp.zeros((1, ENC), jnp.bfloat16)], axis=0)

    def expert_density(packed):
        rows_of, first_mat, second_mat, head_row = packed
        return jax.nn.softplus(forward(padded[rows_of], first_mat, second_mat, head_row)[4])

    density_slots = lax.map(expert_density, (lookup, w_first, w_second, w_head))
    density = density_slots.reshape(-1)[slot_index].reshape(shards, S_DEV)
    absorb = density * step_len
    extinction, _ = jax.vmap(running_sums)(absorb, segment_of)
    misfit = extinction - target
    inclusive, seg_totals = jax.vmap(running_sums)(misfit, segment_of)
    grad_density = (seg_totals - inclusive + misfit) * step_len
    grad_slots = jnp.zeros((EXPERTS * per_expert,), jnp.float32).at[slot_index].set(grad_density.reshape(-1))
    grad_slots = grad_slots.reshape(EXPERTS, per_expert)

    def expert_grads(packed):
        rows_of, grad_in, first_mat, second_mat, head_row = packed
        inputs = padded[rows_of]
        pre_one, act_one, pre_two, act_two, logits = forward(inputs, first_mat, second_mat, head_row)
        grad_logit = grad_in * jax.nn.sigmoid(logits)
        grad_head = jnp.dot(grad_logit.astype(jnp.bfloat16), act_two, preferred_element_type=jnp.float32)
        grad_pre_two = (grad_logit[:, None] * head_row.astype(jnp.float32)[None, :] * silu_slope(pre_two)).astype(jnp.bfloat16)
        grad_second = jnp.dot(act_one.T, grad_pre_two, preferred_element_type=jnp.float32)
        grad_act_one = jnp.dot(grad_pre_two, second_mat.T, preferred_element_type=jnp.float32)
        grad_pre_one = (grad_act_one * silu_slope(pre_one)).astype(jnp.bfloat16)
        grad_first = jnp.dot(inputs.T, grad_pre_one, preferred_element_type=jnp.float32)
        return grad_first.astype(jnp.bfloat16), grad_second.astype(jnp.bfloat16), grad_head.astype(jnp.bfloat16)

    grad_first, grad_second, grad_head = lax.map(expert_grads, (lookup, grad_slots, w_first, w_second, w_head))
    return extinction, grad_first, grad_second, grad_head
```

```python
import functools

import jax
import jax.numpy as jnp
from jax import lax
from jax.experimental import pallas as pl
from jax.experimental.pallas import tpu as pltpu
from jax.sharding import PartitionSpec as P

MESH = pl.DeviceIdType.MESH
ROWS = 8
PLACE = [('d', 0), ('e', 0), ('d', 1), ('e', 1), ('e', 2)]


def up(value, unit):
    return (value + unit - 1) // unit * unit


def nt(a, b):
    return lax.dot_general(a, b, (((1,), (1,)), ((), ())), preferred_element_type=jnp.float32)


def tn(a, b):
    return lax.dot_general(a, b, (((0,), (0,)), ((), ())), preferred_element_type=jnp.float32)


def nn(a, b):
    return jnp.dot(a, b, preferred_element_type=jnp.float32)


def split2(x):
    high = x.astype(jnp.bfloat16)
    low = (x - high.astype(jnp.float32)).astype(jnp.bfloat16)
    return high, low


def one(mask):
    return jnp.where(mask, 1.0, 0.0).astype(jnp.bfloat16)


def kernel(
    cfg,
    feat_h, eof_h, seg_h, step_h, targ_h, w1_h, w2_h, wh_h,
    ext_o, g1_o, g2_o, gh_o,
    feat, eof, seg, step, targ, w1, w2, wh, ins,
    own_s, oh_s, slot_s, rank_s,
    send, recv, msend, mrecv,
    x_s, a1_s, a2_s, sl1_s, hs2_s, gp2_s,
    dens, sig, table, tcol, grads, gsend, grecv, row_s, fore_s, back_s, cf_s, cb_s, acc1, acc2,
    fss, frs, mss, mrs, dss, drs, gss, grs,
):
    NE, ND, EL, S, NB, cap, dcp, G, CH = cfg
    D = NE * ND
    Q = D * ROWS
    NG = D // G
    GR = G * cap
    SPC = CH * G
    NCH = NG // CH
    CR = CH * GR
    nblk = S // NB
    H = D // 2
    le, ld = NE.bit_length() - 1, ND.bit_length() - 1
    keep = D <= 64
    e_me = lax.axis_index("expert")
    d_me = lax.axis_index("dp")
    spots = [("e", i) for i in range(le)]
    spots = PLACE if len(PLACE) == le + ld else [("d", i) for i in range(ld)] + spots

    def flips(j, bit, where):
        mask = where(j < H, H + j, D - 1 - j)
        ke = [None] * le
        kd = [None] * ld
        for i, (axis, w) in enumerate(spots):
            (ke if axis == "e" else kd)[w] = bit(mask, i)
        return ke, kd

    def sbit(v, i):
        return lax.rem(lax.div(v, jnp.int32(1 << i)), jnp.int32(2))

    def vbit(v, i):
        return (v >> i) & 1

    e_bits = [sbit(e_me, i) for i in range(le)]
    d_bits = [sbit(d_me, i) for i in range(ld)]

    def to_dev(j):
        ke, kd = flips(j, sbit, jnp.where)
        e = sum(lax.rem(x + k, jnp.int32(2)) * (1 << i) for i, (x, k) in enumerate(zip(e_bits, ke)))
        d = sum(lax.rem(x + k, jnp.int32(2)) * (1 << i) for i, (x, k) in enumerate(zip(d_bits, kd)))
        return (e, d)

    barrier = pltpu.get_barrier_semaphore()

    def greet(j, c):
        pl.semaphore_signal(barrier, inc=1, device_id=to_dev(j), device_id_type=MESH)
        return c

    lax.fori_loop(0, D - 1, greet, 0)

    arrays = (
        (eof_h, eof), (feat_h.at[0], feat), (seg_h, seg), (step_h, step), (targ_h, targ),
        (w1_h, w1), (w2_h, w2), (wh_h, wh),
    )
    loads = [pltpu.make_async_copy(a, b, ins.at[i]) for i, (a, b) in enumerate(arrays)]
    for load in loads:
        load.start()

    def loop(n, body, init):
        if not keep:
            return lax.fori_loop(0, n, body, init)
        for b in range(n):
            init = body(b, init)
        return init

    qi = lax.broadcasted_iota(jnp.int32, (Q, NB), 0)
    jq = qi >> 3
    mq = qi & (ROWS - 1)
    ke, kd = flips(jq, vbit, jnp.where)
    de = sum(((x + k) & 1) << i for i, (x, k) in enumerate(zip(e_bits, ke)))
    dd = sum(((x + k) & 1) << i for i, (x, k) in enumerate(zip(d_bits, kd)))
    own_s[...] = jnp.where(mq < EL, (de * ND + dd) * EL + mq, -1)

    tri = lax.broadcasted_iota(jnp.int32, (NB, NB + 128), 0) < lax.broadcasted_iota(
        jnp.int32, (NB, NB + 128), 1
    )
    tri = one(jnp.logical_or(tri, lax.broadcasted_iota(jnp.int32, (NB, NB + 128), 1) >= NB))

    def cols(b):
        return pl.ds(b * NB if keep else pl.multiple_of(b * NB, NB), NB)

    def tile(x):
        return jnp.concatenate([x] * (NB // 128), axis=1)

    def hot(b):
        if keep:
            return oh_s[:, cols(b)]
        return one(eof[:, cols(b)] == own_s[...])

    def rank_pass(b, carry):
        hit = eof[:, cols(b)] == own_s[...]
        hits = one(hit)
        if keep:
            oh_s[:, cols(b)] = hits
        full = nn(hits, tri)
        ranks = full[:, :NB] + tile(carry)
        rank_s[:, cols(b)] = jnp.sum(jnp.where(hit, ranks, 0.0), axis=0, keepdims=True)
        return carry + full[:, NB:]

    loads[0].wait()
    counts = loop(nblk, rank_pass, jnp.zeros((Q, 128), jnp.float32))
    q128 = lax.broadcasted_iota(jnp.int32, (Q, 128), 0)
    ends = counts
    for t in range(1, EL):
        ends = ends + jnp.where((q128 & (ROWS - 1)) >= t, pltpu.roll(counts, t, 0), 0.0)
    msend[...] = ends.reshape(D, ROWS, 128)[:, :EL, :]
    base = ((q128 >> 3) * dcp).astype(jnp.float32) + ends - counts
    shift = (((q128 >> 3) & (G - 1)) * cap).astype(jnp.float32)

    def slot_pass(b, c):
        hit = eof[:, cols(b)] == own_s[...]
        rank = rank_s[:, cols(b)]
        at = jnp.sum(jnp.where(hit, tile(base), 0.0), axis=0, keepdims=True) + rank
        slot_s[:, cols(b)] = at.astype(jnp.int32)
        if G > 1:
            rank_s[:, cols(b)] = rank + jnp.sum(
                jnp.where(hit, tile(shift), 0.0), axis=0, keepdims=True
            )
        return c

    loop(nblk, slot_pass, 0)

    pl.semaphore_wait(barrier, D - 1)

    def frows(j):
        return pl.ds(pl.multiple_of(j * dcp, dcp), dcp)

    def meta_copy(j, c):
        pltpu.make_async_remote_copy(
            src_ref=msend.at[j], dst_ref=mrecv.at[j], send_sem=mss, recv_sem=mrs,
            device_id=to_dev(j), device_id_type=MESH,
        ).start()
        return c

    lax.fori_loop(0, D - 1, meta_copy, 0)
    pltpu.make_async_copy(msend.at[D - 1], mrecv.at[D - 1], mrs).start()

    def feature_copy(j):
        pltpu.make_async_remote_copy(
            src_ref=send.at[frows(j)], dst_ref=recv.at[frows(j)],
            send_sem=fss, recv_sem=frs.at[j // SPC],
            device_id=to_dev(j), device_id_type=MESH,
        ).start()

    PK = 2
    PR = PK * dcp

    def pack(p):
        acc = None
        for b in range(S // 256):
            s = slice(b * 256, (b + 1) * 256)
            want = lax.broadcasted_iota(jnp.int32, (PR, 256), 0)
            part = nn(one((slot_s[:, s] - p * PR) == want), feat[s, :])
            acc = part if acc is None else acc + part
        send[pl.ds(pl.multiple_of(p * PR, PR), PR), :] = acc.astype(jnp.bfloat16)

    def pack_send(p, c):
        pack(p)

        feature_copy(p * PK)

        @pl.when(p < D // PK - 1)
        def _():
            feature_copy(p * PK + 1)

        @pl.when(p == D // PK - 1)
        def _():
            mine = frows(D - 1)
            pltpu.make_async_copy(send.at[mine], recv.at[mine], frs.at[NCH - 1]).start()

        return c

    loads[1].wait()
    lax.fori_loop(0, D // PK, pack_send, 0)
    for load in loads[2:]:
        load.wait()

    NR = S // 128
    wide = (NR, 128)
    segs = seg[...]
    pos = lax.broadcasted_iota(jnp.int32, wide, 1)
    row = lax.broadcasted_iota(jnp.int32, wide, 0)
    fore = jnp.ones(wide, jnp.float32)
    back = fore
    for k in range(7):
        s = 1 << k
        same = jnp.logical_and(pltpu.roll(segs, s, 1) == segs, pos >= s)
        fore = fore + jnp.where(same, pltpu.roll(fore, s, 1), 0.0)
        same = jnp.logical_and(pltpu.roll(segs, 128 - s, 1) == segs, pos < 128 - s)
        back = back + jnp.where(same, pltpu.roll(back, 128 - s, 1), 0.0)
    fore_s[...] = fore
    back_s[...] = back
    ends_of = pltpu.roll(jnp.broadcast_to(segs[:, 127:128], wide), 1, 0)
    cf_s[...] = jnp.where(jnp.logical_and(ends_of == segs, row > 0), 1.0, 0.0)
    starts_of = pltpu.roll(jnp.broadcast_to(segs[:, 0:1], wide), NR - 1, 0)
    cb_s[...] = jnp.where(jnp.logical_and(starts_of == segs, row < NR - 1), 1.0, 0.0)

    pltpu.make_async_copy(mrecv, mrecv, mrs).wait()

    lane = lax.broadcasted_iota(jnp.int32, (1, G * dcp), 1)
    lane_g = lane // dcp if G > 1 else None
    lane_j = (lane - lane_g * dcp if G > 1 else lane).astype(jnp.float32)
    sub8 = lax.broadcasted_iota(jnp.int32, (ROWS, 1), 0)

    def forward(i, c):
        ci = jnp.where(i == 0, 0, jnp.where(i <= NCH // 2, i + NCH // 2 - 1, i - NCH // 2))
        span = pl.ds(pl.multiple_of(ci * SPC * dcp, SPC * dcp), SPC * dcp)
        pltpu.make_async_copy(recv.at[span], recv.at[span], frs.at[ci]).wait()
        for g in range(CH):
            grp = ci * CH + g
            targets = [jnp.full((1, G * dcp), -1.0, jnp.float32) for _ in range(EL)]
            for h in range(G):
                m = mrecv[grp * G + h]
                for e in range(EL):
                    lo = m[e - 1 : e, 0:1] if e else jnp.zeros((1, 1), jnp.float32)
                    hi = m[e : e + 1, 0:1]
                    ok = jnp.logical_and(lane_j >= lo, lane_j < hi)
                    if G > 1:
                        ok = jnp.logical_and(ok, lane_g == h)
                    targets[e] = jnp.where(ok, lane_j - lo + h * cap, targets[e])
            want = lax.broadcasted_iota(jnp.int32, (GR, G * dcp), 0).astype(jnp.float32)
            pick = jnp.concatenate([one(t == want) for t in targets], axis=0)
            rows = recv[pl.ds(pl.multiple_of(grp * G * dcp, G * dcp), G * dcp), :]
            x = nn(pick, rows).astype(jnp.bfloat16)
            for e in range(EL):
                x_s[e, pl.ds(pl.multiple_of(grp * GR, GR), GR), :] = x[e * GR : (e + 1) * GR]
        own = pl.ds(pl.multiple_of(ci * CR, CR), CR)
        logit = []
        for e in range(EL):
            p1 = nn(x_s[e, own, :], w1[e])
            s1 = jax.nn.sigmoid(p1)
            a1 = (p1 * s1).astype(jnp.bfloat16)
            a1_s[e, own, :] = a1
            sl1_s[e, own, :] = s1 * (1.0 + p1 * (1.0 - s1))
            p2 = nn(a1, w2[e])
            s2 = jax.nn.sigmoid(p2)
            a2 = (p2 * s2).astype(jnp.bfloat16)
            a2_s[e, own, :] = a2
            head = wh[e : e + 1, :]
            hs2_s[e, own, :] = head.astype(jnp.float32) * (s2 * (1.0 + p2 * (1.0 - s2)))
            logit.append(nt(jnp.broadcast_to(head, (16, head.shape[1])), a2)[:ROWS])
        lg = jnp.zeros((ROWS, CR), jnp.float32)
        for e in range(EL):
            lg = jnp.where(sub8 == e, logit[e], lg)
        den = jnp.maximum(lg, 0.0) + jnp.log1p(jnp.exp(-jnp.abs(lg)))
        sg = jax.nn.sigmoid(lg)
        pad = jnp.zeros((ROWS, 128 - GR), jnp.float32)
        for g in range(CH):
            grp = ci * CH + g
            dens[grp] = jnp.concatenate([den[:, g * GR : (g + 1) * GR], pad], axis=1)[:EL]
            sig[grp] = jnp.concatenate([sg[:, g * GR : (g + 1) * GR], pad], axis=1)

        def give(j, c2):
            @pl.when(j == D - 1)
            def _():
                pltpu.make_async_copy(dens.at[NG - 1], table.at[D - 1], drs).start()

            @pl.when(j < D - 1)
            def _():
                pltpu.make_async_remote_copy(
                    src_ref=dens.at[j // G], dst_ref=table.at[j], send_sem=dss, recv_sem=drs,
                    device_id=to_dev(j), device_id_type=MESH,
                ).start()

            return c2

        lax.fori_loop(ci * SPC, (ci + 1) * SPC, give, 0)
        return c

    lax.fori_loop(0, NCH, forward, 0)

    grads[...] = jnp.zeros_like(grads)
    pltpu.make_async_copy(table, table, drs).wait()
    grads[:, 0:EL, :] = table[...]
    tt = grads[...].reshape(Q, 128).T[:GR]
    th, tl = split2(tt)
    tcol[0:GR, :] = th
    tcol[GR : 2 * GR, :] = tl

    def line(b, t):
        at = b * (NB // 128) + t
        return slice(at, at + 1) if keep else pl.ds(at, 1)

    def put(b, x):
        for t in range(NB // 128):
            row_s[line(b, t), :] = x[:, t * 128 : (t + 1) * 128]

    def take(b):
        return jnp.concatenate([row_s[line(b, t), :] for t in range(NB // 128)], axis=1)

    def spread(b, c):
        both = nn(tcol[...], hot(b))
        both = both[:GR] + both[GR:]
        want = lax.broadcasted_iota(jnp.int32, (GR, NB), 0).astype(jnp.float32)
        put(b, jnp.sum(jnp.where(rank_s[:, cols(b)] == want, both, 0.0), axis=0, keepdims=True))
        return c

    loop(nblk, spread, 0)

    steps = step[...]
    run = row_s[...] * steps
    before = fore_s[...]
    for k in range(7):
        s = 1 << k
        run = run + jnp.where(before > s, pltpu.roll(run, s, 1), 0.0)
    tail = pltpu.roll(jnp.broadcast_to(run[:, 127:128], wide), 1, 0)
    run = run + jnp.where(cf_s[...] > 0.0, tail, 0.0)
    ext_o[...] = run
    run = run - targ[...]
    after = back_s[...]
    for k in range(7):
        s = 1 << k
        run = run + jnp.where(after > s, pltpu.roll(run, 128 - s, 1), 0.0)
    head = pltpu.roll(jnp.broadcast_to(run[:, 0:1], wide), NR - 1, 0)
    run = run + jnp.where(cb_s[...] > 0.0, head, 0.0)
    row_s[...] = run * steps

    def collect(b, total):
        want = lax.broadcasted_iota(jnp.int32, (GR, NB), 0).astype(jnp.float32)
        held = jnp.where(rank_s[:, cols(b)] == want, take(b), 0.0)
        both = jnp.concatenate(split2(held), axis=0)
        return total + nt(hot(b), both)

    got = loop(nblk, collect, jnp.zeros((Q, 2 * GR), jnp.float32))
    got = got[:, :GR] + got[:, GR:]
    got = jnp.concatenate([got, jnp.zeros((Q, 128 - GR), jnp.float32)], axis=1)
    gsend[...] = got.reshape(D, ROWS, 128)[:, :EL, :]

    def grad_copy(j, c):
        pltpu.make_async_remote_copy(
            src_ref=gsend.at[j], dst_ref=grecv.at[j], send_sem=gss, recv_sem=grs.at[j // H],
            device_id=to_dev(j), device_id_type=MESH,
        ).start()
        return c

    lax.fori_loop(0, H, lambda j, c: grad_copy(H - 1 - j, c), 0)
    lax.fori_loop(H, D - 1, grad_copy, 0)
    pltpu.make_async_copy(gsend.at[D - 1], grecv.at[D - 1], grs.at[1]).start()

    RH = NG * GR // 2

    def backward(h, heads):
        got = grecv.at[pl.ds(h * H, H)]
        pltpu.make_async_copy(got, got, grs.at[h]).wait()
        for ci in range(h * NCH // 2, (h + 1) * NCH // 2):
            parts = []
            for g in range(CH):
                grp = ci * CH + g
                tot = grecv[grp * G]
                for t in range(1, G):
                    tot = tot + grecv[grp * G + t]
                parts.append(jnp.concatenate([tot, tot], axis=0)[:ROWS] * sig[grp])
            gt = jnp.concatenate(parts, axis=0).T[:GR]
            gb = jnp.concatenate([p[:, :GR] for p in parts], axis=1)
            gb = jnp.concatenate([gb, gb], axis=0).astype(jnp.bfloat16)
            for e in range(EL):
                for g in range(CH):
                    at = (ci * CH + g) * GR
                    rows = slice(at, at + GR)
                    q = g * ROWS + e
                    gp2_s[e, rows, :] = (gt[:, q : q + 1] * hs2_s[e, rows, :]).astype(jnp.bfloat16)
                heads[e] = heads[e] + nn(gb, a2_s[e, ci * CR : (ci + 1) * CR, :])
        half = slice(h * RH, (h + 1) * RH)
        for e in range(EL):
            gp2 = gp2_s[e, half, :]
            d2 = tn(a1_s[e, half, :], gp2)
            gp1 = (nt(gp2, w2[e]) * sl1_s[e, half, :]).astype(jnp.bfloat16)
            d1 = tn(x_s[e, half, :], gp1)
            if h:
                acc2[e] = d2
                acc1[e] = d1
            else:
                g2_o[e] = (acc2[e] + d2).astype(jnp.bfloat16)
                g1_o[e] = (acc1[e] + d1).astype(jnp.bfloat16)
        return heads

    heads = [jnp.zeros((2 * ROWS, w1.shape[2]), jnp.float32) for _ in range(EL)]
    heads = backward(0, backward(1, heads))
    for e in range(EL):
        gh_o[e : e + 1, :] = heads[e][e : e + 1].astype(jnp.bfloat16)

    sent = pl.ds(0, (D - 1) * dcp)
    pltpu.make_async_copy(send.at[sent], send.at[sent], fss).wait()
    rest = pl.ds(0, D - 1)
    pltpu.make_async_copy(msend.at[rest], msend.at[rest], mss).wait()
    pltpu.make_async_copy(table.at[rest], table.at[rest], dss).wait()
    pltpu.make_async_copy(gsend.at[rest], gsend.at[rest], gss).wait()


def hand_on(*refs):
    half = len(refs) // 2
    for source, to in zip(refs[:half], refs[half:]):
        to[...] = source[...]


def local(ne, nd, features, expert_of, segment_of, step_len, target, w_first, w_second, w_head):
    EL, F, H = w_first.shape
    S = features.shape[1]
    D = ne * nd
    cap = max(3, (2 * S + D * EL - 1) // (D * EL))
    dcp = up(3 * cap, 16)
    G = 1 if cap % 16 == 0 else 16
    NG = D // G
    CH = 4 if NG % 4 == 0 else 1
    NCH = NG // CH
    NB = 256 if D <= 64 else 128
    GR = G * cap
    Q = D * ROWS
    cfg = (ne, nd, EL, S, NB, cap, dcp, G, CH)
    bf, f32, i32 = jnp.bfloat16, jnp.float32, jnp.int32
    V = pltpu.VMEM
    dma = pltpu.SemaphoreType.DMA
    R = NG * GR
    NR = S // 128
    rows = (NR, 128)
    vm = pl.BlockSpec(memory_space=pltpu.VMEM)
    outs = pl.pallas_call(
        functools.partial(kernel, cfg),
        out_shape=(
            jax.ShapeDtypeStruct((NR, 128), f32),
            jax.ShapeDtypeStruct((EL, F, H), bf),
            jax.ShapeDtypeStruct((EL, H, H), bf),
            jax.ShapeDtypeStruct((EL, H), bf),
        ),
        in_specs=[pl.BlockSpec(memory_space=pl.ANY)] * 8,
        out_specs=(vm,) * 4,
        scratch_shapes=[
            V((S, F), bf), V((1, S), i32), V(rows, i32), V(rows, f32), V(rows, f32),
            V((EL, F, H), bf), V((EL, H, H), bf), V((EL, H), bf), dma((8,)),
            V((Q, NB), i32), V((Q, S if D <= 64 else 128), bf), V((1, S), i32), V((1, S), f32),
            V((D * dcp, F), bf), V((D * dcp, F), bf), V((D, EL, 128), f32), V((D, EL, 128), f32),
            V((EL, R, F), bf), V((EL, R, H), bf), V((EL, R, H), bf), V((EL, R, H), f32),
            V((EL, R, H), f32), V((EL, R, H), bf),
            V((NG, EL, 128), f32), V((NG, ROWS, 128), f32), V((D, EL, 128), f32),
            V((2 * GR, Q), bf), V((D, ROWS, 128), f32), V((D, EL, 128), f32), V((D, EL, 128), f32), V(rows, f32), V(rows, f32), V(rows, f32),
            V(rows, f32), V(rows, f32), V((EL, F, H), f32), V((EL, H, H), f32),
            dma, dma((NCH,)), dma, dma, dma, dma, dma, dma((2,)),
        ],
        compiler_params=pltpu.CompilerParams(
            collective_id=0, has_side_effects=True, vmem_limit_bytes=67043328
        ),
    )(
        features, expert_of.reshape(1, S), segment_of.reshape(rows), step_len.reshape(rows),
        target.reshape(rows), w_first, w_second, w_head
    )
    ext, *grads = pl.pallas_call(
        hand_on,
        out_shape=tuple(jax.ShapeDtypeStruct(o.shape, o.dtype) for o in outs),
        in_specs=[vm] * 4,
        out_specs=(vm,) * 4,
    )(*outs)
    return ext.reshape(1, S), *grads


def solution(mesh):
    sizes = dict(mesh.shape)
    both = ("expert", "dp")
    three, two = P(both, None, None), P(both, None)
    return jax.shard_map(
        functools.partial(local, sizes["expert"], sizes["dp"]),
        mesh=mesh,
        in_specs=(three, three, two, two, two, three, three, two),
        out_specs=(two, three, three, two),
        check_vma=False,
    )
```

```python
import functools

import jax
import jax.numpy as jnp
from jax import lax
from jax.experimental import pallas as pl
from jax.experimental.pallas import tpu as pltpu
from jax.sharding import PartitionSpec as P

MESH = pl.DeviceIdType.MESH
ROWS = 8
STEPS = ((1, 4), (4, 4), (16, 4), (64, 2))
ORDER = (6, 7, 4, 0, 1, 5, 2, 3)
PLACE = [('d', 0), ('e', 0), ('d', 1), ('e', 1), ('e', 2)]


def up(value, unit):
    return (value + unit - 1) // unit * unit


def nt(a, b):
    return lax.dot_general(a, b, (((1,), (1,)), ((), ())), preferred_element_type=jnp.float32)


def tn(a, b):
    return lax.dot_general(a, b, (((0,), (0,)), ((), ())), preferred_element_type=jnp.float32)


def nn(a, b):
    return jnp.dot(a, b, preferred_element_type=jnp.float32)


def split2(x):
    high = x.astype(jnp.bfloat16)
    low = (x - high.astype(jnp.float32)).astype(jnp.bfloat16)
    return high, low


def one(mask):
    return jnp.where(mask, 1.0, 0.0).astype(jnp.bfloat16)


def kernel(
    cfg,
    feat_h, eof_h, seg_h, step_h, targ_h, w1_h, w2_h, wh_h,
    ext_o, g1_o, g2_o, gh_o,
    feat, eof, seg, step, targ, w1, w2, wh, ins,
    own_s, oh_s, slot_s, rank_s,
    send, recv, msend, mrecv,
    x_s, a1_s, a2_s, sl1_s, hs2_s, gp2_s, gp1_s,
    dens, sig, table, tcol, grads, gsend, grecv, row_s, fore_s, back_s, cf_s, cb_s, acc1, acc2,
    fss, frs, mss, mrs, dss, drs, gss, grs,
):
    NE, ND, EL, S, NB, cap, dcp, G, CH = cfg
    D = NE * ND
    Q = D * ROWS
    NG = D // G
    GR = G * cap
    SPC = CH * G
    NCH = NG // CH
    CR = CH * GR
    nblk = S // NB
    H = D // 2
    le, ld = NE.bit_length() - 1, ND.bit_length() - 1
    keep = D <= 64
    e_me = lax.axis_index("expert")
    d_me = lax.axis_index("dp")
    spots = [("e", i) for i in range(le)]
    spots = PLACE if len(PLACE) == le + ld else [("d", i) for i in range(ld)] + spots

    def flips(j, bit, where):
        mask = where(j < H, H + j, D - 1 - j)
        ke = [None] * le
        kd = [None] * ld
        for i, (axis, w) in enumerate(spots):
            (ke if axis == "e" else kd)[w] = bit(mask, i)
        return ke, kd

    def sbit(v, i):
        return lax.rem(lax.div(v, jnp.int32(1 << i)), jnp.int32(2))

    def vbit(v, i):
        return (v >> i) & 1

    e_bits = [sbit(e_me, i) for i in range(le)]
    d_bits = [sbit(d_me, i) for i in range(ld)]

    def to_dev(j):
        ke, kd = flips(j, sbit, jnp.where)
        e = sum(lax.rem(x + k, jnp.int32(2)) * (1 << i) for i, (x, k) in enumerate(zip(e_bits, ke)))
        d = sum(lax.rem(x + k, jnp.int32(2)) * (1 << i) for i, (x, k) in enumerate(zip(d_bits, kd)))
        return (e, d)

    barrier = pltpu.get_barrier_semaphore()

    def greet(j, c):
        pl.semaphore_signal(barrier, inc=1, device_id=to_dev(j), device_id_type=MESH)
        return c

    lax.fori_loop(0, D - 1, greet, 0)

    arrays = (
        (eof_h, eof), (feat_h.at[0], feat), (seg_h, seg), (step_h, step), (targ_h, targ),
        (w1_h, w1), (w2_h, w2), (wh_h, wh),
    )
    loads = [pltpu.make_async_copy(a, b, ins.at[i]) for i, (a, b) in enumerate(arrays)]
    for load in loads:
        load.start()

    def loop(n, body, init):
        if not keep:
            return lax.fori_loop(0, n, body, init)
        for b in range(n):
            init = body(b, init)
        return init

    qi = lax.broadcasted_iota(jnp.int32, (Q, NB), 0)
    jq = qi >> 3
    mq = qi & (ROWS - 1)
    ke, kd = flips(jq, vbit, jnp.where)
    de = sum(((x + k) & 1) << i for i, (x, k) in enumerate(zip(e_bits, ke)))
    dd = sum(((x + k) & 1) << i for i, (x, k) in enumerate(zip(d_bits, kd)))
    own_s[...] = jnp.where(mq < EL, (de * ND + dd) * EL + mq, -1)

    tri = lax.broadcasted_iota(jnp.int32, (NB, NB + 128), 0) < lax.broadcasted_iota(
        jnp.int32, (NB, NB + 128), 1
    )
    tri = one(jnp.logical_or(tri, lax.broadcasted_iota(jnp.int32, (NB, NB + 128), 1) >= NB))

    def cols(b):
        return pl.ds(b * NB if keep else pl.multiple_of(b * NB, NB), NB)

    def tile(x):
        return jnp.concatenate([x] * (NB // 128), axis=1)

    def hot(b):
        if keep:
            return oh_s[:, cols(b)]
        return one(eof[:, cols(b)] == own_s[...])

    def rank_pass(b, carry):
        hit = eof[:, cols(b)] == own_s[...]
        hits = one(hit)
        if keep:
            oh_s[:, cols(b)] = hits
        full = nn(hits, tri)
        ranks = full[:, :NB] + tile(carry)
        rank_s[:, cols(b)] = jnp.sum(jnp.where(hit, ranks, 0.0), axis=0, keepdims=True)
        return carry + full[:, NB:]

    loads[0].wait()
    counts = loop(nblk, rank_pass, jnp.zeros((Q, 128), jnp.float32))
    q128 = lax.broadcasted_iota(jnp.int32, (Q, 128), 0)
    ends = counts
    for t in range(1, EL):
        ends = ends + jnp.where((q128 & (ROWS - 1)) >= t, pltpu.roll(counts, t, 0), 0.0)
    msend[...] = ends.reshape(D, ROWS, 128)[:, :EL, :]
    base = ((q128 >> 3) * dcp).astype(jnp.float32) + ends - counts
    shift = (((q128 >> 3) & (G - 1)) * cap).astype(jnp.float32)

    def slot_pass(b, c):
        hit = eof[:, cols(b)] == own_s[...]
        rank = rank_s[:, cols(b)]
        at = jnp.sum(jnp.where(hit, tile(base), 0.0), axis=0, keepdims=True) + rank
        slot_s[:, cols(b)] = at.astype(jnp.int32)
        if G > 1:
            rank_s[:, cols(b)] = rank + jnp.sum(
                jnp.where(hit, tile(shift), 0.0), axis=0, keepdims=True
            )
        return c

    loop(nblk, slot_pass, 0)

    pl.semaphore_wait(barrier, D - 1)

    def frows(j):
        return pl.ds(pl.multiple_of(j * dcp, dcp), dcp)

    def meta_copy(j, c):
        pltpu.make_async_remote_copy(
            src_ref=msend.at[j], dst_ref=mrecv.at[j], send_sem=mss, recv_sem=mrs,
            device_id=to_dev(j), device_id_type=MESH,
        ).start()
        return c

    lax.fori_loop(0, D - 1, meta_copy, 0)
    pltpu.make_async_copy(msend.at[D - 1], mrecv.at[D - 1], mrs).start()

    def feature_copy(j):
        pltpu.make_async_remote_copy(
            src_ref=send.at[frows(j)], dst_ref=recv.at[frows(j)],
            send_sem=fss, recv_sem=frs.at[j // SPC],
            device_id=to_dev(j), device_id_type=MESH,
        ).start()

    PK = 2
    PR = PK * dcp

    def pack(p):
        acc = None
        for b in range(S // 256):
            s = slice(b * 256, (b + 1) * 256)
            want = lax.broadcasted_iota(jnp.int32, (PR, 256), 0)
            part = nn(one((slot_s[:, s] - p * PR) == want), feat[s, :])
            acc = part if acc is None else acc + part
        send[pl.ds(pl.multiple_of(p * PR, PR), PR), :] = acc.astype(jnp.bfloat16)

    def pack_send(p, c):
        pack(p)

        feature_copy(p * PK)

        @pl.when(p < D // PK - 1)
        def _():
            feature_copy(p * PK + 1)

        @pl.when(p == D // PK - 1)
        def _():
            mine = frows(D - 1)
            pltpu.make_async_copy(send.at[mine], recv.at[mine], frs.at[NCH - 1]).start()

        return c

    loads[1].wait()
    lax.fori_loop(0, D // PK, pack_send, 0)
    for load in loads[2:]:
        load.wait()

    NR = S // 128
    wide = (NR, 128)
    segs = seg[...]
    pos = lax.broadcasted_iota(jnp.int32, wide, 1)
    row = lax.broadcasted_iota(jnp.int32, wide, 0)
    fore = jnp.ones(wide, jnp.float32)
    back = fore
    for k in range(7):
        s = 1 << k
        same = jnp.logical_and(pltpu.roll(segs, s, 1) == segs, pos >= s)
        fore = fore + jnp.where(same, pltpu.roll(fore, s, 1), 0.0)
        same = jnp.logical_and(pltpu.roll(segs, 128 - s, 1) == segs, pos < 128 - s)
        back = back + jnp.where(same, pltpu.roll(back, 128 - s, 1), 0.0)
    fore_s[...] = fore
    back_s[...] = back
    ends_of = pltpu.roll(jnp.broadcast_to(segs[:, 127:128], wide), 1, 0)
    cf_s[...] = jnp.where(jnp.logical_and(ends_of == segs, row > 0), 1.0, 0.0)
    starts_of = pltpu.roll(jnp.broadcast_to(segs[:, 0:1], wide), NR - 1, 0)
    cb_s[...] = jnp.where(jnp.logical_and(starts_of == segs, row < NR - 1), 1.0, 0.0)

    pltpu.make_async_copy(mrecv, mrecv, mrs).wait()

    lane = lax.broadcasted_iota(jnp.int32, (1, G * dcp), 1)
    lane_g = lane // dcp if G > 1 else None
    lane_j = (lane - lane_g * dcp if G > 1 else lane).astype(jnp.float32)
    sub8 = lax.broadcasted_iota(jnp.int32, (ROWS, 1), 0)

    def chunk_at(i):
        part = max(NCH // 8, 1)
        block = lax.div(i, jnp.int32(part))
        at = jnp.int32(ORDER[0] if NCH >= 8 else 0)
        for k, v in enumerate(ORDER):
            at = jnp.where(block == k, v, at)
        return at * part + lax.rem(i, jnp.int32(part)) if NCH >= 8 else i

    def forward(i, c):
        ci = chunk_at(i)
        span = pl.ds(pl.multiple_of(ci * SPC * dcp, SPC * dcp), SPC * dcp)
        pltpu.make_async_copy(recv.at[span], recv.at[span], frs.at[ci]).wait()
        for g in range(CH):
            grp = ci * CH + g
            targets = [jnp.full((1, G * dcp), -1.0, jnp.float32) for _ in range(EL)]
            for h in range(G):
                m = mrecv[grp * G + h]
                for e in range(EL):
                    lo = m[e - 1 : e, 0:1] if e else jnp.zeros((1, 1), jnp.float32)
                    hi = m[e : e + 1, 0:1]
                    ok = jnp.logical_and(lane_j >= lo, lane_j < hi)
                    if G > 1:
                        ok = jnp.logical_and(ok, lane_g == h)
                    targets[e] = jnp.where(ok, lane_j - lo + h * cap, targets[e])
            want = lax.broadcasted_iota(jnp.int32, (GR, G * dcp), 0).astype(jnp.float32)
            pick = jnp.concatenate([one(t == want) for t in targets], axis=0)
            rows = recv[pl.ds(pl.multiple_of(grp * G * dcp, G * dcp), G * dcp), :]
            x = nn(pick, rows).astype(jnp.bfloat16)
            for e in range(EL):
                x_s[e, pl.ds(pl.multiple_of(grp * GR, GR), GR), :] = x[e * GR : (e + 1) * GR]
        own = pl.ds(pl.multiple_of(ci * CR, CR), CR)
        logit = []
        for e in range(EL):
            p1 = nn(x_s[e, own, :], w1[e])
            s1 = jax.nn.sigmoid(p1)
            a1 = (p1 * s1).astype(jnp.bfloat16)
            a1_s[e, own, :] = a1
            sl1_s[e, own, :] = s1 * (1.0 + p1 * (1.0 - s1))
            p2 = nn(a1, w2[e])
            s2 = jax.nn.sigmoid(p2)
            a2 = (p2 * s2).astype(jnp.bfloat16)
            a2_s[e, own, :] = a2
            head = wh[e : e + 1, :]
            hs2_s[e, own, :] = head.astype(jnp.float32) * (s2 * (1.0 + p2 * (1.0 - s2)))
            logit.append(nt(jnp.broadcast_to(head, (16, head.shape[1])), a2)[:ROWS])
        lg = jnp.zeros((ROWS, CR), jnp.float32)
        for e in range(EL):
            lg = jnp.where(sub8 == e, logit[e], lg)
        den = jnp.maximum(lg, 0.0) + jnp.log1p(jnp.exp(-jnp.abs(lg)))
        sg = jax.nn.sigmoid(lg)
        pad = jnp.zeros((ROWS, 128 - GR), jnp.float32)
        for g in range(CH):
            grp = ci * CH + g
            dens[grp] = jnp.concatenate([den[:, g * GR : (g + 1) * GR], pad], axis=1)[:EL]
            sig[grp] = jnp.concatenate([sg[:, g * GR : (g + 1) * GR], pad], axis=1)

        def give(j, c2):
            @pl.when(j == D - 1)
            def _():
                pltpu.make_async_copy(dens.at[NG - 1], table.at[D - 1], drs).start()

            @pl.when(j < D - 1)
            def _():
                pltpu.make_async_remote_copy(
                    src_ref=dens.at[j // G], dst_ref=table.at[j], send_sem=dss, recv_sem=drs,
                    device_id=to_dev(j), device_id_type=MESH,
                ).start()

            return c2

        lax.fori_loop(ci * SPC, (ci + 1) * SPC, give, 0)
        return c

    RH = NG * GR // 2

    def prepare(h):
        half = slice(h * RH, (h + 1) * RH)
        for e in range(EL):
            back_one = nt(hs2_s[e, half, :].astype(jnp.bfloat16), w2[e])
            sl1_s[e, half, :] = sl1_s[e, half, :] * back_one

    last = 2 * max(NCH // 8, 1) if NCH >= 8 else 0
    lax.fori_loop(0, NCH - last, forward, 0)
    if last:
        prepare(1)
        lax.fori_loop(NCH - last, NCH, forward, 0)
    else:
        prepare(1)
    prepare(0)

    grads[...] = jnp.zeros_like(grads)
    pltpu.make_async_copy(table, table, drs).wait()
    grads[:, 0:EL, :] = table[...]
    tt = grads[...].reshape(Q, 128).T[:GR]
    th, tl = split2(tt)
    tcol[0:GR, :] = th
    tcol[GR : 2 * GR, :] = tl

    def line(b, t):
        at = b * (NB // 128) + t
        return slice(at, at + 1) if keep else pl.ds(at, 1)

    def put(b, x):
        for t in range(NB // 128):
            row_s[line(b, t), :] = x[:, t * 128 : (t + 1) * 128]

    def take(b):
        return jnp.concatenate([row_s[line(b, t), :] for t in range(NB // 128)], axis=1)

    def spread(b, c):
        both = nn(tcol[...], hot(b))
        both = both[:GR] + both[GR:]
        want = lax.broadcasted_iota(jnp.int32, (GR, NB), 0).astype(jnp.float32)
        put(b, jnp.sum(jnp.where(rank_s[:, cols(b)] == want, both, 0.0), axis=0, keepdims=True))
        return c

    loop(nblk, spread, 0)

    steps = step[...]
    run = row_s[...] * steps
    before = fore_s[...]
    for s, times in STEPS:
        run = run + sum(
            jnp.where(before > t * s, pltpu.roll(run, t * s, 1), 0.0) for t in range(1, times)
        )
    tail = pltpu.roll(jnp.broadcast_to(run[:, 127:128], wide), 1, 0)
    run = run + jnp.where(cf_s[...] > 0.0, tail, 0.0)
    ext_o[...] = run
    run = run - targ[...]
    after = back_s[...]
    for s, times in STEPS:
        run = run + sum(
            jnp.where(after > t * s, pltpu.roll(run, 128 - t * s, 1), 0.0) for t in range(1, times)
        )
    head = pltpu.roll(jnp.broadcast_to(run[:, 0:1], wide), NR - 1, 0)
    run = run + jnp.where(cb_s[...] > 0.0, head, 0.0)
    row_s[...] = run * steps

    def collect(b, total):
        want = lax.broadcasted_iota(jnp.int32, (GR, NB), 0).astype(jnp.float32)
        held = jnp.where(rank_s[:, cols(b)] == want, take(b), 0.0)
        both = jnp.concatenate(split2(held), axis=0)
        return total + nt(hot(b), both)

    got = loop(nblk, collect, jnp.zeros((Q, 2 * GR), jnp.float32))
    got = got[:, :GR] + got[:, GR:]
    got = jnp.concatenate([got, jnp.zeros((Q, 128 - GR), jnp.float32)], axis=1)
    gsend[...] = got.reshape(D, ROWS, 128)[:, :EL, :]

    def grad_copy(j, c):
        pltpu.make_async_remote_copy(
            src_ref=gsend.at[j], dst_ref=grecv.at[j], send_sem=gss, recv_sem=grs.at[j // H],
            device_id=to_dev(j), device_id_type=MESH,
        ).start()
        return c

    lax.fori_loop(0, H, lambda j, c: grad_copy(H - 1 - j, c), 0)
    lax.fori_loop(H, D - 1, grad_copy, 0)
    pltpu.make_async_copy(gsend.at[D - 1], grecv.at[D - 1], grs.at[1]).start()

    def backward(h, heads):
        got = grecv.at[pl.ds(h * H, H)]
        pltpu.make_async_copy(got, got, grs.at[h]).wait()
        for ci in range(h * NCH // 2, (h + 1) * NCH // 2):
            parts = []
            for g in range(CH):
                grp = ci * CH + g
                tot = grecv[grp * G]
                for t in range(1, G):
                    tot = tot + grecv[grp * G + t]
                parts.append(jnp.concatenate([tot, tot], axis=0)[:ROWS] * sig[grp])
            gt = jnp.concatenate(parts, axis=0).T[:GR]
            gb = jnp.concatenate([p[:, :GR] for p in parts], axis=1)
            gb = jnp.concatenate([gb, gb], axis=0).astype(jnp.bfloat16)
            for e in range(EL):
                for g in range(CH):
                    at = (ci * CH + g) * GR
                    rows = slice(at, at + GR)
                    q = g * ROWS + e
                    col = gt[:, q : q + 1]
                    gp2_s[e, rows, :] = (col * hs2_s[e, rows, :]).astype(jnp.bfloat16)
                    gp1_s[e, rows, :] = (col * sl1_s[e, rows, :]).astype(jnp.bfloat16)
                heads[e] = heads[e] + nn(gb, a2_s[e, ci * CR : (ci + 1) * CR, :])
        half = slice(h * RH, (h + 1) * RH)
        for e in range(EL):
            d2 = tn(a1_s[e, half, :], gp2_s[e, half, :])
            d1 = tn(x_s[e, half, :], gp1_s[e, half, :])
            if h:
                acc2[e] = d2
                acc1[e] = d1
            else:
                g2_o[e] = (acc2[e] + d2).astype(jnp.bfloat16)
                g1_o[e] = (acc1[e] + d1).astype(jnp.bfloat16)
        return heads

    heads = [jnp.zeros((2 * ROWS, w1.shape[2]), jnp.float32) for _ in range(EL)]
    heads = backward(0, backward(1, heads))
    for e in range(EL):
        gh_o[e : e + 1, :] = heads[e][e : e + 1].astype(jnp.bfloat16)

    sent = pl.ds(0, (D - 1) * dcp)
    pltpu.make_async_copy(send.at[sent], send.at[sent], fss).wait()
    rest = pl.ds(0, D - 1)
    pltpu.make_async_copy(msend.at[rest], msend.at[rest], mss).wait()
    pltpu.make_async_copy(table.at[rest], table.at[rest], dss).wait()
    pltpu.make_async_copy(gsend.at[rest], gsend.at[rest], gss).wait()


def hand_on(*refs):
    *refs, sems = refs
    half = len(refs) // 2
    copies = [
        pltpu.make_async_copy(source, to, sems.at[i])
        for i, (source, to) in enumerate(zip(refs[:half], refs[half:]))
    ]
    for copy in copies:
        copy.start()
    for copy in copies:
        copy.wait()


def local(ne, nd, features, expert_of, segment_of, step_len, target, w_first, w_second, w_head):
    EL, F, H = w_first.shape
    S = features.shape[1]
    D = ne * nd
    cap = max(3, (2 * S + D * EL - 1) // (D * EL))
    dcp = up(3 * cap, 16)
    G = 1 if cap % 16 == 0 else 16
    NG = D // G
    CH = 2 if NG % 16 == 0 else 1
    NCH = NG // CH
    NB = 256 if D <= 64 else 128
    GR = G * cap
    Q = D * ROWS
    cfg = (ne, nd, EL, S, NB, cap, dcp, G, CH)
    bf, f32, i32 = jnp.bfloat16, jnp.float32, jnp.int32
    V = pltpu.VMEM
    dma = pltpu.SemaphoreType.DMA
    R = NG * GR
    NR = S // 128
    rows = (NR, 128)
    vm = pl.BlockSpec(memory_space=pltpu.VMEM)
    outs = pl.pallas_call(
        functools.partial(kernel, cfg),
        out_shape=(
            jax.ShapeDtypeStruct((NR, 128), f32),
            jax.ShapeDtypeStruct((EL, F, H), bf),
            jax.ShapeDtypeStruct((EL, H, H), bf),
            jax.ShapeDtypeStruct((EL, H), bf),
        ),
        in_specs=[pl.BlockSpec(memory_space=pltpu.HBM)] * 8,
        out_specs=(vm,) * 4,
        scratch_shapes=[
            V((S, F), bf), V((1, S), i32), V(rows, i32), V(rows, f32), V(rows, f32),
            V((EL, F, H), bf), V((EL, H, H), bf), V((EL, H), bf), dma((8,)),
            V((Q, NB), i32), V((Q, S if D <= 64 else 128), bf), V((1, S), i32), V((1, S), f32),
            V((D * dcp, F), bf), V((D * dcp, F), bf), V((D, EL, 128), f32), V((D, EL, 128), f32),
            V((EL, R, F), bf), V((EL, R, H), bf), V((EL, R, H), bf), V((EL, R, H), f32),
            V((EL, R, H), f32), V((EL, R, H), bf), V((EL, R, H), bf),
            V((NG, EL, 128), f32), V((NG, ROWS, 128), f32), V((D, EL, 128), f32),
            V((2 * GR, Q), bf), V((D, ROWS, 128), f32), V((D, EL, 128), f32), V((D, EL, 128), f32), V(rows, f32), V(rows, f32), V(rows, f32),
            V(rows, f32), V(rows, f32), V((EL, F, H), f32), V((EL, H, H), f32),
            dma, dma((NCH,)), dma, dma, dma, dma, dma, dma((2,)),
        ],
        compiler_params=pltpu.CompilerParams(
            collective_id=0, has_side_effects=True, vmem_limit_bytes=52 * 1024 * 1024
        ),
    )(
        *[pltpu.with_memory_space_constraint(x, pltpu.HBM) for x in (features, expert_of.reshape(1, S), segment_of.reshape(rows), step_len.reshape(rows),
        target.reshape(rows), w_first, w_second, w_head)]
    )
    ext, *grads = pl.pallas_call(
        hand_on,
        out_shape=tuple(jax.ShapeDtypeStruct(o.shape, o.dtype) for o in outs),
        in_specs=[vm] * 4,
        out_specs=(pl.BlockSpec(memory_space=pltpu.HBM),) * 4,
        scratch_shapes=[dma((4,))],
        compiler_params=pltpu.CompilerParams(vmem_limit_bytes=4 * 1024 * 1024),
    )(*outs)
    return ext.reshape(1, S), *grads


def solution(mesh):
    sizes = dict(mesh.shape)
    both = ("expert", "dp")
    three, two = P(both, None, None), P(both, None)
    return jax.shard_map(
        functools.partial(local, sizes["expert"], sizes["dp"]),
        mesh=mesh,
        in_specs=(three, three, two, two, two, three, three, two),
        out_specs=(two, three, three, two),
        check_vma=False,
    )
```

```python
import functools

import jax
import jax.numpy as jnp
from jax import lax
from jax.experimental import pallas as pl
from jax.experimental.pallas import tpu as pltpu
from jax.sharding import PartitionSpec as P

MESH = pl.DeviceIdType.MESH
ROWS = 8
EARLY = 1
STEPS = ((1, 4), (4, 4), (16, 4), (64, 2))
ORDER = (6, 7, 4, 0, 1, 5, 2, 3)
PLACE = [('d', 0), ('e', 0), ('d', 1), ('e', 1), ('e', 2)]


def up(value, unit):
    return (value + unit - 1) // unit * unit


def nt(a, b):
    return lax.dot_general(a, b, (((1,), (1,)), ((), ())), preferred_element_type=jnp.float32)


def tn(a, b):
    return lax.dot_general(a, b, (((0,), (0,)), ((), ())), preferred_element_type=jnp.float32)


def nn(a, b):
    return jnp.dot(a, b, preferred_element_type=jnp.float32)


def split2(x):
    high = x.astype(jnp.bfloat16)
    low = (x - high.astype(jnp.float32)).astype(jnp.bfloat16)
    return high, low


def one(mask):
    return jnp.where(mask, 1.0, 0.0).astype(jnp.bfloat16)


def kernel(
    cfg,
    feat_h, eof_h, seg_h, step_h, targ_h, w1_h, w2_h, wh_h,
    ext_o, g1_o, g2_o, gh_o,
    feat, eof, seg, step, targ, w1, w2, wh, ins,
    own_s, oh_s, slot_s, rank_s,
    send, recv, msend, mrecv,
    x_s, a1_s, a2_s, sl1_s, hs2_s, gp2_s, gp1_s,
    dens, sig, table, tcol, grads, gsend, grecv, row_s, fore_s, back_s, cf_s, cb_s, acc1, acc2,
    fss, frs, mss, mrs, dss, drs, gss, grs,
):
    NE, ND, EL, S, NB, cap, dcp, G, CH = cfg
    D = NE * ND
    Q = D * ROWS
    NG = D // G
    GR = G * cap
    SPC = CH * G
    NCH = NG // CH
    CR = CH * GR
    nblk = S // NB
    H = D // 2
    le, ld = NE.bit_length() - 1, ND.bit_length() - 1
    keep = D <= 64
    e_me = lax.axis_index("expert")
    d_me = lax.axis_index("dp")
    spots = [("e", i) for i in range(le)]
    spots = PLACE if len(PLACE) == le + ld else [("d", i) for i in range(ld)] + spots

    def flips(j, bit, where):
        mask = where(j < H, H + j, D - 1 - j)
        ke = [None] * le
        kd = [None] * ld
        for i, (axis, w) in enumerate(spots):
            (ke if axis == "e" else kd)[w] = bit(mask, i)
        return ke, kd

    def sbit(v, i):
        return lax.rem(lax.div(v, jnp.int32(1 << i)), jnp.int32(2))

    def vbit(v, i):
        return (v >> i) & 1

    e_bits = [sbit(e_me, i) for i in range(le)]
    d_bits = [sbit(d_me, i) for i in range(ld)]

    def to_dev(j):
        if isinstance(j, int):
            mask = H + j if j < H else D - 1 - j
            e, d = jnp.int32(0), jnp.int32(0)
            for i, (axis, w) in enumerate(spots):
                bit = (e_bits if axis == "e" else d_bits)[w]
                bit = (1 - bit if mask >> i & 1 else bit) * (1 << w)
                e, d = (e + bit, d) if axis == "e" else (e, d + bit)
            return (e, d)
        ke, kd = flips(j, sbit, jnp.where)
        e = sum(lax.rem(x + k, jnp.int32(2)) * (1 << i) for i, (x, k) in enumerate(zip(e_bits, ke)))
        d = sum(lax.rem(x + k, jnp.int32(2)) * (1 << i) for i, (x, k) in enumerate(zip(d_bits, kd)))
        return (e, d)

    barrier = pltpu.get_barrier_semaphore()

    def each(low, high, f):
        if keep:
            for j in range(low, high):
                f(j)
        else:
            lax.fori_loop(low, high, lambda j, c: (f(j), c)[1], 0)

    def greet(j):
        pl.semaphore_signal(barrier, inc=1, device_id=to_dev(j), device_id_type=MESH)

    each(0, H, lambda j: greet(H - 1 - j))
    each(H, D - 1, greet)

    arrays = (
        (eof_h, eof), (feat_h.at[0], feat), (seg_h, seg), (step_h, step), (targ_h, targ),
        (w1_h, w1), (w2_h, w2), (wh_h, wh),
    )
    loads = [pltpu.make_async_copy(a, b, ins.at[i]) for i, (a, b) in enumerate(arrays)]
    for load in loads:
        load.start()

    def loop(n, body, init):
        if not keep:
            return lax.fori_loop(0, n, body, init)
        for b in range(n):
            init = body(b, init)
        return init

    qi = lax.broadcasted_iota(jnp.int32, (Q, NB), 0)
    jq = qi >> 3
    mq = qi & (ROWS - 1)
    ke, kd = flips(jq, vbit, jnp.where)
    de = sum(((x + k) & 1) << i for i, (x, k) in enumerate(zip(e_bits, ke)))
    dd = sum(((x + k) & 1) << i for i, (x, k) in enumerate(zip(d_bits, kd)))
    own_s[...] = jnp.where(mq < EL, (de * ND + dd) * EL + mq, -1)

    tri = lax.broadcasted_iota(jnp.int32, (NB, NB + 128), 0) < lax.broadcasted_iota(
        jnp.int32, (NB, NB + 128), 1
    )
    tri = one(jnp.logical_or(tri, lax.broadcasted_iota(jnp.int32, (NB, NB + 128), 1) >= NB))

    def cols(b):
        return pl.ds(b * NB if keep else pl.multiple_of(b * NB, NB), NB)

    def tile(x):
        return jnp.concatenate([x] * (NB // 128), axis=1)

    def hot(b):
        if keep:
            return oh_s[:, cols(b)]
        return one(eof[:, cols(b)] == own_s[...])

    def rank_pass(b, carry):
        hit = eof[:, cols(b)] == own_s[...]
        hits = one(hit)
        if keep:
            oh_s[:, cols(b)] = hits
        full = nn(hits, tri)
        ranks = full[:, :NB] + tile(carry)
        rank_s[:, cols(b)] = jnp.sum(jnp.where(hit, ranks, 0.0), axis=0, keepdims=True)
        return carry + full[:, NB:]

    loads[0].wait()
    counts = loop(nblk, rank_pass, jnp.zeros((Q, 128), jnp.float32))
    q128 = lax.broadcasted_iota(jnp.int32, (Q, 128), 0)
    ends = counts
    for t in range(1, EL):
        ends = ends + jnp.where((q128 & (ROWS - 1)) >= t, pltpu.roll(counts, t, 0), 0.0)
    msend[...] = ends.reshape(D, ROWS, 128)[:, :EL, :]
    base = ((q128 >> 3) * dcp).astype(jnp.float32) + ends - counts
    shift = (((q128 >> 3) & (G - 1)) * cap).astype(jnp.float32)

    def slot_pass(b, c):
        hit = eof[:, cols(b)] == own_s[...]
        rank = rank_s[:, cols(b)]
        at = jnp.sum(jnp.where(hit, tile(base), 0.0), axis=0, keepdims=True) + rank
        slot_s[:, cols(b)] = at.astype(jnp.int32)
        if G > 1:
            rank_s[:, cols(b)] = rank + jnp.sum(
                jnp.where(hit, tile(shift), 0.0), axis=0, keepdims=True
            )
        return c

    loop(nblk, slot_pass, 0)

    PK = 2
    PR = PK * dcp

    def frows(j):
        return pl.ds(j * dcp if isinstance(j, int) else pl.multiple_of(j * dcp, dcp), dcp)

    def feature_copy(j):
        pltpu.make_async_remote_copy(
            src_ref=send.at[frows(j)], dst_ref=recv.at[frows(j)],
            send_sem=fss, recv_sem=frs.at[j // SPC],
            device_id=to_dev(j), device_id_type=MESH,
        ).start()

    def meta_copy(j):
        pltpu.make_async_remote_copy(
            src_ref=msend.at[j], dst_ref=mrecv.at[j], send_sem=mss, recv_sem=mrs,
            device_id=to_dev(j), device_id_type=MESH,
        ).start()

    def pack(p):
        acc = None
        for b in range(S // 256):
            s = slice(b * 256, (b + 1) * 256)
            want = lax.broadcasted_iota(jnp.int32, (PR, 256), 0)
            part = nn(one((slot_s[:, s] - p * PR) == want), feat[s, :])
            acc = part if acc is None else acc + part
        send[pl.ds(pl.multiple_of(p * PR, PR), PR), :] = acc.astype(jnp.bfloat16)

    def pack_send(p, c):
        pack(p)
        feature_copy(p * PK)
        feature_copy(p * PK + 1)
        return c

    loads[1].wait()
    lax.fori_loop(0, EARLY, lambda p, c: (pack(p), c)[1], 0)
    pl.semaphore_wait(barrier, D - 1)
    each(0, D - 1, meta_copy)
    pltpu.make_async_copy(msend.at[D - 1], mrecv.at[D - 1], mrs).start()
    for j in range(EARLY * PK):
        feature_copy(j)
    lax.fori_loop(EARLY, D // PK - 1, pack_send, 0)
    pack(jnp.int32(D // PK - 1))
    feature_copy(D - 2)
    mine = frows(D - 1)
    pltpu.make_async_copy(send.at[mine], recv.at[mine], frs.at[NCH - 1]).start()
    for load in loads[2:]:
        load.wait()

    NR = S // 128
    wide = (NR, 128)
    segs = seg[...]
    pos = lax.broadcasted_iota(jnp.int32, wide, 1)
    row = lax.broadcasted_iota(jnp.int32, wide, 0)
    fore = jnp.ones(wide, jnp.float32)
    back = fore
    for k in range(7):
        s = 1 << k
        same = jnp.logical_and(pltpu.roll(segs, s, 1) == segs, pos >= s)
        fore = fore + jnp.where(same, pltpu.roll(fore, s, 1), 0.0)
        same = jnp.logical_and(pltpu.roll(segs, 128 - s, 1) == segs, pos < 128 - s)
        back = back + jnp.where(same, pltpu.roll(back, 128 - s, 1), 0.0)
    fore_s[...] = fore
    back_s[...] = back
    ends_of = pltpu.roll(jnp.broadcast_to(segs[:, 127:128], wide), 1, 0)
    cf_s[...] = jnp.where(jnp.logical_and(ends_of == segs, row > 0), 1.0, 0.0)
    starts_of = pltpu.roll(jnp.broadcast_to(segs[:, 0:1], wide), NR - 1, 0)
    cb_s[...] = jnp.where(jnp.logical_and(starts_of == segs, row < NR - 1), 1.0, 0.0)

    pltpu.make_async_copy(mrecv, mrecv, mrs).wait()

    lane = lax.broadcasted_iota(jnp.int32, (1, G * dcp), 1)
    lane_g = lane // dcp if G > 1 else None
    lane_j = (lane - lane_g * dcp if G > 1 else lane).astype(jnp.float32)
    sub8 = lax.broadcasted_iota(jnp.int32, (ROWS, 1), 0)

    def chunk_at(i):
        part = max(NCH // 8, 1)
        block = lax.div(i, jnp.int32(part))
        at = jnp.int32(ORDER[0] if NCH >= 8 else 0)
        for k, v in enumerate(ORDER):
            at = jnp.where(block == k, v, at)
        return at * part + lax.rem(i, jnp.int32(part)) if NCH >= 8 else i

    def forward(i, c):
        ci = chunk_at(i)
        span = pl.ds(pl.multiple_of(ci * SPC * dcp, SPC * dcp), SPC * dcp)
        pltpu.make_async_copy(recv.at[span], recv.at[span], frs.at[ci]).wait()
        for g in range(CH):
            grp = ci * CH + g
            targets = [jnp.full((1, G * dcp), -1.0, jnp.float32) for _ in range(EL)]
            for h in range(G):
                m = mrecv[grp * G + h]
                for e in range(EL):
                    lo = m[e - 1 : e, 0:1] if e else jnp.zeros((1, 1), jnp.float32)
                    hi = m[e : e + 1, 0:1]
                    ok = jnp.logical_and(lane_j >= lo, lane_j < hi)
                    if G > 1:
                        ok = jnp.logical_and(ok, lane_g == h)
                    targets[e] = jnp.where(ok, lane_j - lo + h * cap, targets[e])
            want = lax.broadcasted_iota(jnp.int32, (GR, G * dcp), 0).astype(jnp.float32)
            pick = jnp.concatenate([one(t == want) for t in targets], axis=0)
            rows = recv[pl.ds(pl.multiple_of(grp * G * dcp, G * dcp), G * dcp), :]
            x = nn(pick, rows).astype(jnp.bfloat16)
            for e in range(EL):
                x_s[e, pl.ds(pl.multiple_of(grp * GR, GR), GR), :] = x[e * GR : (e + 1) * GR]
        own = pl.ds(pl.multiple_of(ci * CR, CR), CR)
        logit = []
        for e in range(EL):
            p1 = nn(x_s[e, own, :], w1[e])
            s1 = jax.nn.sigmoid(p1)
            a1 = (p1 * s1).astype(jnp.bfloat16)
            a1_s[e, own, :] = a1
            sl1_s[e, own, :] = s1 * (1.0 + p1 * (1.0 - s1))
            p2 = nn(a1, w2[e])
            s2 = jax.nn.sigmoid(p2)
            a2 = (p2 * s2).astype(jnp.bfloat16)
            a2_s[e, own, :] = a2
            head = wh[e : e + 1, :]
            hs2_s[e, own, :] = head.astype(jnp.float32) * (s2 * (1.0 + p2 * (1.0 - s2)))
            logit.append(nt(jnp.broadcast_to(head, (16, head.shape[1])), a2)[:ROWS])
        lg = jnp.zeros((ROWS, CR), jnp.float32)
        for e in range(EL):
            lg = jnp.where(sub8 == e, logit[e], lg)
        den = jnp.maximum(lg, 0.0) + jnp.log1p(jnp.exp(-jnp.abs(lg)))
        sg = jax.nn.sigmoid(lg)
        pad = jnp.zeros((ROWS, 128 - GR), jnp.float32)
        for g in range(CH):
            grp = ci * CH + g
            dens[grp] = jnp.concatenate([den[:, g * GR : (g + 1) * GR], pad], axis=1)[:EL]
            sig[grp] = jnp.concatenate([sg[:, g * GR : (g + 1) * GR], pad], axis=1)

        def give(j, c2):
            @pl.when(j == D - 1)
            def _():
                pltpu.make_async_copy(dens.at[NG - 1], table.at[D - 1], drs).start()

            @pl.when(j < D - 1)
            def _():
                pltpu.make_async_remote_copy(
                    src_ref=dens.at[j // G], dst_ref=table.at[j], send_sem=dss, recv_sem=drs,
                    device_id=to_dev(j), device_id_type=MESH,
                ).start()

            return c2

        lax.fori_loop(ci * SPC, (ci + 1) * SPC, give, 0)
        return c

    RH = NG * GR // 2

    def prepare(h):
        half = slice(h * RH, (h + 1) * RH)
        for e in range(EL):
            back_one = nt(hs2_s[e, half, :].astype(jnp.bfloat16), w2[e])
            sl1_s[e, half, :] = sl1_s[e, half, :] * back_one

    last = 2 * max(NCH // 8, 1) if NCH >= 8 else 0
    lax.fori_loop(0, NCH - last, forward, 0)
    if last:
        prepare(1)
        lax.fori_loop(NCH - last, NCH, forward, 0)
    else:
        prepare(1)
    prepare(0)

    grads[...] = jnp.zeros_like(grads)
    pltpu.make_async_copy(table, table, drs).wait()
    grads[:, 0:EL, :] = table[...]
    tt = grads[...].reshape(Q, 128).T[:GR]
    th, tl = split2(tt)
    tcol[0:GR, :] = th
    tcol[GR : 2 * GR, :] = tl

    def line(b, t):
        at = b * (NB // 128) + t
        return slice(at, at + 1) if keep else pl.ds(at, 1)

    def put(b, x):
        for t in range(NB // 128):
            row_s[line(b, t), :] = x[:, t * 128 : (t + 1) * 128]

    def take(b):
        return jnp.concatenate([row_s[line(b, t), :] for t in range(NB // 128)], axis=1)

    def spread(b, c):
        both = nn(tcol[...], hot(b))
        both = both[:GR] + both[GR:]
        want = lax.broadcasted_iota(jnp.int32, (GR, NB), 0).astype(jnp.float32)
        put(b, jnp.sum(jnp.where(rank_s[:, cols(b)] == want, both, 0.0), axis=0, keepdims=True))
        return c

    loop(nblk, spread, 0)

    steps = step[...]
    run = row_s[...] * steps
    before = fore_s[...]
    for s, times in STEPS:
        run = run + sum(
            jnp.where(before > t * s, pltpu.roll(run, t * s, 1), 0.0) for t in range(1, times)
        )
    tail = pltpu.roll(jnp.broadcast_to(run[:, 127:128], wide), 1, 0)
    run = run + jnp.where(cf_s[...] > 0.0, tail, 0.0)
    ext_o[...] = run
    run = run - targ[...]
    after = back_s[...]
    for s, times in STEPS:
        run = run + sum(
            jnp.where(after > t * s, pltpu.roll(run, 128 - t * s, 1), 0.0) for t in range(1, times)
        )
    head = pltpu.roll(jnp.broadcast_to(run[:, 0:1], wide), NR - 1, 0)
    run = run + jnp.where(cb_s[...] > 0.0, head, 0.0)
    row_s[...] = run * steps

    def collect(b, total):
        want = lax.broadcasted_iota(jnp.int32, (GR, NB), 0).astype(jnp.float32)
        held = jnp.where(rank_s[:, cols(b)] == want, take(b), 0.0)
        both = jnp.concatenate(split2(held), axis=0)
        return total + nt(hot(b), both)

    got = loop(nblk, collect, jnp.zeros((Q, 2 * GR), jnp.float32))
    got = got[:, :GR] + got[:, GR:]
    got = jnp.concatenate([got, jnp.zeros((Q, 128 - GR), jnp.float32)], axis=1)
    gsend[...] = got.reshape(D, ROWS, 128)[:, :EL, :]

    def grad_copy(j):
        pltpu.make_async_remote_copy(
            src_ref=gsend.at[j], dst_ref=grecv.at[j], send_sem=gss, recv_sem=grs.at[j // H],
            device_id=to_dev(j), device_id_type=MESH,
        ).start()

    each(0, H, lambda j: grad_copy(H - 1 - j))
    each(H, D - 1, grad_copy)
    pltpu.make_async_copy(gsend.at[D - 1], grecv.at[D - 1], grs.at[1]).start()

    def backward(h, heads):
        got = grecv.at[pl.ds(h * H, H)]
        pltpu.make_async_copy(got, got, grs.at[h]).wait()
        for ci in range(h * NCH // 2, (h + 1) * NCH // 2):
            parts = []
            for g in range(CH):
                grp = ci * CH + g
                tot = grecv[grp * G]
                for t in range(1, G):
                    tot = tot + grecv[grp * G + t]
                parts.append(jnp.concatenate([tot, tot], axis=0)[:ROWS] * sig[grp])
            gt = jnp.concatenate(parts, axis=0).T[:GR]
            gb = jnp.concatenate([p[:, :GR] for p in parts], axis=1)
            gb = jnp.concatenate([gb, gb], axis=0).astype(jnp.bfloat16)
            for e in range(EL):
                for g in range(CH):
                    at = (ci * CH + g) * GR
                    rows = slice(at, at + GR)
                    q = g * ROWS + e
                    col = gt[:, q : q + 1]
                    gp2_s[e, rows, :] = (col * hs2_s[e, rows, :]).astype(jnp.bfloat16)
                    gp1_s[e, rows, :] = (col * sl1_s[e, rows, :]).astype(jnp.bfloat16)
                heads[e] = heads[e] + nn(gb, a2_s[e, ci * CR : (ci + 1) * CR, :])
        half = slice(h * RH, (h + 1) * RH)
        for e in range(EL):
            d2 = tn(a1_s[e, half, :], gp2_s[e, half, :])
            d1 = tn(x_s[e, half, :], gp1_s[e, half, :])
            if h:
                acc2[e] = d2
                acc1[e] = d1
            else:
                g2_o[e] = (acc2[e] + d2).astype(jnp.bfloat16)
                g1_o[e] = (acc1[e] + d1).astype(jnp.bfloat16)
        return heads

    heads = [jnp.zeros((2 * ROWS, w1.shape[2]), jnp.float32) for _ in range(EL)]
    heads = backward(0, backward(1, heads))
    for e in range(EL):
        gh_o[e : e + 1, :] = heads[e][e : e + 1].astype(jnp.bfloat16)

    sent = pl.ds(0, (D - 1) * dcp)
    pltpu.make_async_copy(send.at[sent], send.at[sent], fss).wait()
    rest = pl.ds(0, D - 1)
    pltpu.make_async_copy(msend.at[rest], msend.at[rest], mss).wait()
    pltpu.make_async_copy(table.at[rest], table.at[rest], dss).wait()
    pltpu.make_async_copy(gsend.at[rest], gsend.at[rest], gss).wait()


def hand_on(*refs):
    *refs, sems = refs
    half = len(refs) // 2
    copies = [
        pltpu.make_async_copy(source, to, sems.at[i])
        for i, (source, to) in enumerate(zip(refs[:half], refs[half:]))
    ]
    for copy in copies:
        copy.start()
    for copy in copies:
        copy.wait()


def local(ne, nd, features, expert_of, segment_of, step_len, target, w_first, w_second, w_head):
    EL, F, H = w_first.shape
    S = features.shape[1]
    D = ne * nd
    cap = max(3, (2 * S + D * EL - 1) // (D * EL))
    dcp = up(3 * cap, 16)
    G = 1 if cap % 16 == 0 else 16
    NG = D // G
    CH = 2 if NG % 16 == 0 else 1
    NCH = NG // CH
    NB = 256 if D <= 64 else 128
    GR = G * cap
    Q = D * ROWS
    cfg = (ne, nd, EL, S, NB, cap, dcp, G, CH)
    bf, f32, i32 = jnp.bfloat16, jnp.float32, jnp.int32
    V = pltpu.VMEM
    dma = pltpu.SemaphoreType.DMA
    R = NG * GR
    NR = S // 128
    rows = (NR, 128)
    vm = pl.BlockSpec(memory_space=pltpu.VMEM)
    outs = pl.pallas_call(
        functools.partial(kernel, cfg),
        out_shape=(
            jax.ShapeDtypeStruct((NR, 128), f32),
            jax.ShapeDtypeStruct((EL, F, H), bf),
            jax.ShapeDtypeStruct((EL, H, H), bf),
            jax.ShapeDtypeStruct((EL, H), bf),
        ),
        in_specs=[pl.BlockSpec(memory_space=pltpu.HBM)] * 8,
        out_specs=(vm,) * 4,
        scratch_shapes=[
            V((S, F), bf), V((1, S), i32), V(rows, i32), V(rows, f32), V(rows, f32),
            V((EL, F, H), bf), V((EL, H, H), bf), V((EL, H), bf), dma((8,)),
            V((Q, NB), i32), V((Q, S if D <= 64 else 128), bf), V((1, S), i32), V((1, S), f32),
            V((D * dcp, F), bf), V((D * dcp, F), bf), V((D, EL, 128), f32), V((D, EL, 128), f32),
            V((EL, R, F), bf), V((EL, R, H), bf), V((EL, R, H), bf), V((EL, R, H), f32),
            V((EL, R, H), f32), V((EL, R, H), bf), V((EL, R, H), bf),
            V((NG, EL, 128), f32), V((NG, ROWS, 128), f32), V((D, EL, 128), f32),
            V((2 * GR, Q), bf), V((D, ROWS, 128), f32), V((D, EL, 128), f32), V((D, EL, 128), f32), V(rows, f32), V(rows, f32), V(rows, f32),
            V(rows, f32), V(rows, f32), V((EL, F, H), f32), V((EL, H, H), f32),
            dma, dma((NCH,)), dma, dma, dma, dma, dma, dma((2,)),
        ],
        compiler_params=pltpu.CompilerParams(
            collective_id=0, has_side_effects=True, vmem_limit_bytes=52 * 1024 * 1024
        ),
    )(
        *[pltpu.with_memory_space_constraint(x, pltpu.HBM) for x in (features, expert_of.reshape(1, S), segment_of.reshape(rows), step_len.reshape(rows),
        target.reshape(rows), w_first, w_second, w_head)]
    )
    ext, *grads = pl.pallas_call(
        hand_on,
        out_shape=tuple(jax.ShapeDtypeStruct(o.shape, o.dtype) for o in outs),
        in_specs=[vm] * 4,
        out_specs=(pl.BlockSpec(memory_space=pltpu.HBM),) * 4,
        scratch_shapes=[dma((4,))],
        compiler_params=pltpu.CompilerParams(vmem_limit_bytes=4 * 1024 * 1024),
    )(*outs)
    return ext.reshape(1, S), *grads


def solution(mesh):
    sizes = dict(mesh.shape)
    both = ("expert", "dp")
    three, two = P(both, None, None), P(both, None)
    return jax.shard_map(
        functools.partial(local, sizes["expert"], sizes["dp"]),
        mesh=mesh,
        in_specs=(three, three, two, two, two, three, three, two),
        out_specs=(two, three, three, two),
        check_vma=False,
    )
```
